256 devices in a mesh: frame: 16 (over y, z_hi, core), row: 16 (over x, z_lo).
Axes of the slice: x: 4, y: 4, z: 8 (z_hi: 2, z_lo: 4; z = z_hi * 4 + z_lo), core: 2. Of those that a mesh axis runs over, the one named last changes fastest.
Arguments:
- spatial_q: bfloat16 [32, 128, 32, 1152], P('frame', 'row'), may hold values from -10.5 to 10.5
- spatial_k: bfloat16 [32, 128, 32, 1152], P('frame', 'row'), may hold values from -10.5 to 10.5
- spatial_v: bfloat16 [32, 128, 32, 1152], P('frame', 'row'), may hold values from -6 to 6
- residual: bfloat16 [32, 128, 32, 1152], P('frame', 'row'), may hold values from -6 to 6
- neighbour_list: int32 [64, 6], P('row'), may hold values from 0 to 15, as said below
- block_mask: int32 [8, 8], replicated, may hold values from 0 to 1, as said below
- out_weight: bfloat16 [1152, 1152], P('frame'), may hold values from -0.1875 to 0.1875
- qkv_weight: bfloat16 [1152, 3456], P('frame'), may hold values from -1.4799 to 1.4799
- pos_embed: float32 [32, 1152], P('frame'), may hold values from -150.5 to 150.5
- mod_shift: float32 [1152], replicated, may hold values from -2 to 2
- mod_scale: float32 [1152], replicated, may hold values from -2 to 2
Outputs:
- temporal_mix: bfloat16 [32, 128, 32, 1152], P('frame', 'row')
The draws below stay inside these ranges and needn't reach their ends.
Inputs may be any that keep to these rules, and one draw needn't show every extreme that they name: `neighbour_list`: each row holds 6 different tiles of its own clip: slot 0 is the row's own tile; every other lies at most one tile row and at most two tile columns away from it, inside the grid of 16 tiles. `block_mask`: entry (i, j) is 1 where i == j and 0 where j > i.
All inputs are finite; a program needn't handle non-finite values.
Results may differ from the reference program's by a relative error of at most 0.0056.
The reference program's roundings to bfloat16 on the way count: a program that leaves them out, or rounds other values in their place, can miss the bound.
Values may be sent and summed in bfloat16 or wider, within the bound.
No kernel may reach another device: no remote copies, remote signals or barrier semaphores. Data moves between devices by JAX's collectives and lax.ppermute only.
A program may use at most 128 MiB of HBM per device.

```python
import math
import jax
import jax.numpy as jnp
from jax import lax

D = 1152
HEADS = 16
TILE = 8
SLOTS = 6
ROWS = 32
COLS = 32
BLOCK = 4
FRAMES = 32
CLIPS = 4
TILES_WIDE = 4
TILES = 16
BLOCKS = 8


def spatial_pair(key):
    full_shape = (FRAMES, CLIPS * ROWS, COLS, D)
    key_q, key_k = jax.random.split(jax.random.fold_in(key, 11))
    queries = jnp.clip(jax.random.normal(key_q, full_shape, jnp.float32), -4.0, 4.0)
    key_draw = jnp.clip(jax.random.normal(key_k, full_shape, jnp.float32), -4.0, 4.0)
    return (queries, key_draw)


def draw_spatial_q(key, part):
    return spatial_pair(key)[0].astype(jnp.bfloat16)


def draw_spatial_k(key, part):
    return spatial_pair(key)[1].astype(jnp.bfloat16)


def draw_qkv_weight(key, part):
    key_w = jax.random.fold_in(key, 23)
    drawn = jnp.clip(jax.random.normal(key_w, (D, 3 * D), jnp.float32), -6.0, 6.0) * D ** (-0.5)
    return drawn.astype(jnp.bfloat16)


def draw_pos_embed(key, part):
    key_a = jax.random.fold_in(jax.random.fold_in(key, 37), 0)
    return jnp.clip(jax.random.normal(key_a, (FRAMES, D), jnp.float32), -4.0, 4.0)


def draw_block_mask(key, part):
    bits = jax.random.randint(jax.random.fold_in(key, 31), (BLOCKS, BLOCKS), 0, 2)
    later = jnp.arange(BLOCKS)[:, None]
    earlier = jnp.arange(BLOCKS)[None, :]
    return jnp.where(later == earlier, 1, jnp.where(later > earlier, bits, 0)).astype(jnp.int32)


def draw_neighbour_list(key, part):
    row_step = jnp.array([-1, -1, -1, -1, -1, 0, 0, 0, 0, 1, 1, 1, 1, 1], jnp.int32)
    col_step = jnp.array([-2, -1, 0, 1, 2, -2, -1, 1, 2, -2, -1, 0, 1, 2], jnp.int32)
    list_rows = jnp.arange(CLIPS * TILES, dtype=jnp.int32)
    tile_row = (list_rows // TILES_WIDE + 1) % (TILES // TILES_WIDE)
    tile_col = list_rows % TILES_WIDE
    tile_ids = tile_row * TILES_WIDE + tile_col
    cand_row = tile_row[:, None] + row_step[None, :]
    cand_col = tile_col[:, None] + col_step[None, :]
    inside = (cand_row >= 0) & (cand_row < TILES // TILES_WIDE) & (cand_col >= 0) & (cand_col < TILES_WIDE)
    scores = jax.random.randint(jax.random.fold_in(key, 41), (CLIPS * TILES, 14), 0, 1 << 20) * 16 + jnp.arange(14, dtype=jnp.int32)[None, :]
    scores = jnp.where(inside, scores, scores + (1 << 26))
    ranking = jnp.argsort(scores, axis=1)[:, :SLOTS - 1]
    chosen = jnp.take_along_axis(cand_row * TILES_WIDE + cand_col, ranking, axis=1)
    return jnp.concatenate([tile_ids[:, None], chosen], axis=1).astype(jnp.int32)


def block_levels(key, shape, cuts, smallest, largest):
    loudness = 1.0
    for axis_at, blocks in cuts:
        draws = jax.random.uniform(jax.random.fold_in(jax.random.fold_in(key, 6), axis_at), (blocks,), jnp.float32, smallest / len(cuts), largest / len(cuts))
        loudness = loudness * jnp.repeat(jnp.exp(draws), shape[axis_at] // blocks).reshape((-1,) + (1,) * (len(shape) - 1 - axis_at))
    return loudness


def gaussian(key, dims, scale, bound, shards=(), kind=jnp.bfloat16):
    values = scale * jax.random.normal(key, dims, jnp.float32)
    if shards:
        values = values * block_levels(key, dims, shards, -0.22, 0.18)
    return jnp.clip(values, -bound, bound).astype(kind)


def setup_inputs(seed: int = 0) -> dict:
    key_list = jax.random.split(jax.random.key(seed), 12)
    spatial_q = draw_spatial_q(jax.random.fold_in(key_list[11], 71), 0)
    spatial_k = draw_spatial_k(jax.random.fold_in(key_list[11], 71), 0)
    spatial_v = gaussian(key_list[2], (FRAMES, CLIPS * ROWS, COLS, D), 1.0, 6.0, ((0, 16), (1, 16)))
    residual = gaussian(key_list[3], (FRAMES, CLIPS * ROWS, COLS, D), 1.0, 6.0, ((0, 16), (1, 16)))
    neighbour_list = draw_neighbour_list(jax.random.fold_in(key_list[11], 71), 0)
    block_mask = draw_block_mask(jax.random.fold_in(key_list[11], 71), 0)
    out_weight = gaussian(key_list[6], (D, D), D ** -0.5, 0.1875, ((0, 16),))
    qkv_weight = draw_qkv_weight(jax.random.fold_in(key_list[11], 71), 0)
    pos_embed = draw_pos_embed(jax.random.fold_in(key_list[11], 71), 0)
    mod_shift = gaussian(key_list[9], (D,), 0.5, 2.0, (), jnp.float32)
    mod_scale = gaussian(key_list[10], (D,), 0.5, 2.0, (), jnp.float32)
    return dict(spatial_q=spatial_q, spatial_k=spatial_k, spatial_v=spatial_v, residual=residual, neighbour_list=neighbour_list, block_mask=block_mask, out_weight=out_weight, qkv_weight=qkv_weight, pos_embed=pos_embed, mod_shift=mod_shift, mod_scale=mod_scale)


EPS = 1e-06

def tiles_of(field):
    leading = field.shape[:-3]
    height, breadth, channels = field.shape[-3:]
    tile_grid = field.reshape(leading + (height // TILE, TILE, breadth // TILE, TILE, channels))
    lead_count = len(leading)
    arrangement = tuple(range(lead_count)) + (lead_count, lead_count + 2, lead_count + 1, lead_count + 3, lead_count + 4)
    tile_grid = jnp.transpose(tile_grid, arrangement)
    return tile_grid.reshape(leading + (height // TILE * (breadth // TILE), TILE * TILE, channels))

def untile(tiles, height, breadth):
    leading = tiles.shape[:-3]
    channels = tiles.shape[-1]
    tile_grid = tiles.reshape(leading + (height // TILE, breadth // TILE, TILE, TILE, channels))
    lead_count = len(leading)
    arrangement = tuple(range(lead_count)) + (lead_count, lead_count + 2, lead_count + 1, lead_count + 3, lead_count + 4)
    return jnp.transpose(tile_grid, arrangement).reshape(leading + (height, breadth, channels))

def window_attention(queries, keys, values):
    tile_count, token_count, channels = queries.shape
    head_size = channels // HEADS
    shaped_q = queries.astype(jnp.float32).reshape(tile_count, token_count, HEADS, head_size)
    shaped_k = keys.astype(jnp.float32).reshape(tile_count, -1, HEADS, head_size)
    shaped_v = values.astype(jnp.float32).reshape(tile_count, -1, HEADS, head_size)
    scores = jnp.einsum('tqhe,tkhe->thqk', shaped_q, shaped_k) * (1.0 / math.sqrt(head_size))
    peak = lax.optimization_barrier(jnp.max(scores, axis=-1, keepdims=True))
    powers = jnp.exp(scores - peak)
    weights = (powers / lax.optimization_barrier(jnp.sum(powers, axis=-1, keepdims=True))).astype(jnp.bfloat16)
    weights = lax.optimization_barrier(weights)
    mixed = jnp.einsum('thqk,tkhe->tqhe', weights.astype(jnp.float32), shaped_v)
    return mixed.astype(jnp.bfloat16).reshape(tile_count, token_count, channels)

def frame_attention(queries, keys, values, allowed):
    frame_count, spot_count, channels = queries.shape
    head_size = channels // HEADS
    shaped_q = queries.astype(jnp.float32).reshape(frame_count, spot_count, HEADS, head_size)
    shaped_k = keys.astype(jnp.float32).reshape(frame_count, spot_count, HEADS, head_size)
    shaped_v = values.astype(jnp.float32).reshape(frame_count, spot_count, HEADS, head_size)
    scores = jnp.einsum('fphe,gphe->phfg', shaped_q, shaped_k) * (1.0 / math.sqrt(head_size))
    scores = jnp.where(allowed, scores, -jnp.inf)
    peak = lax.optimization_barrier(jnp.max(scores, axis=-1, keepdims=True))
    powers = jnp.exp(scores - peak)
    weights = (powers / lax.optimization_barrier(jnp.sum(powers, axis=-1, keepdims=True))).astype(jnp.bfloat16)
    weights = lax.optimization_barrier(weights)
    mixed = jnp.einsum('phfg,gphe->fphe', weights.astype(jnp.float32), shaped_v)
    return mixed.astype(jnp.bfloat16).reshape(frame_count, spot_count, channels)

def normalize(field, mod_shift, mod_scale):
    average = lax.optimization_barrier(jnp.mean(field, axis=-1, keepdims=True))
    centred = field - average
    spread = lax.optimization_barrier(jnp.mean(centred * centred, axis=-1, keepdims=True))
    return centred * lax.rsqrt(spread + EPS) * (1.0 + mod_scale) + mod_shift

def by_clip(field):
    rolled = jnp.roll(field, TILE, axis=1)
    shaped = rolled.reshape(FRAMES, CLIPS, ROWS, COLS, D)
    return jnp.transpose(shaped, (1, 0, 2, 3, 4))

def reference(spatial_q, spatial_k, spatial_v, residual, neighbour_list, block_mask, out_weight, qkv_weight, pos_embed, mod_shift, mod_scale):
    allowed = jnp.repeat(jnp.repeat(block_mask, BLOCK, axis=0), BLOCK, axis=1) == 1
    spots = ROWS * COLS
    block_spots = TILE * COLS

    def clip_pass(clip_items):
        clip_q, clip_k, clip_v, clip_x, clip_list = clip_items

        def spatial_frame(items):
            frame_q, frame_k, frame_v, frame_x, frame_pos = items
            tiles_q = tiles_of(frame_q)
            tiles_k = jnp.take(tiles_of(frame_k), clip_list, axis=0).reshape(TILES, SLOTS * TILE * TILE, D)
            tiles_v = jnp.take(tiles_of(frame_v), clip_list, axis=0).reshape(TILES, SLOTS * TILE * TILE, D)
            heads = untile(window_attention(tiles_q, tiles_k, tiles_v), ROWS, COLS).reshape(ROWS * COLS, D)
            spatial_sum = jnp.dot(heads, out_weight, preferred_element_type=jnp.float32)
            mixed = (frame_x.reshape(ROWS * COLS, D).astype(jnp.float32) + spatial_sum).astype(jnp.bfloat16)
            mixed = lax.optimization_barrier(mixed)
            shifted = mixed.astype(jnp.float32) + frame_pos[None, :]
            return normalize(shifted, mod_shift, mod_scale).astype(jnp.bfloat16)
        normed_all = lax.map(spatial_frame, (clip_q, clip_k, clip_v, clip_x, pos_embed))
        grouped = jnp.transpose(normed_all.reshape(FRAMES, spots // block_spots, block_spots, D), (1, 0, 2, 3))

        def temporal_block(rows_block):
            projected = jnp.dot(rows_block.reshape(-1, D), qkv_weight, preferred_element_type=jnp.float32).astype(jnp.bfloat16)
            projected = lax.optimization_barrier(projected)
            projected = projected.reshape(FRAMES, block_spots, 3 * D)
            return frame_attention(projected[..., :D], projected[..., D:2 * D], projected[..., 2 * D:], allowed)
        mixed_blocks = lax.map(temporal_block, grouped)
        return jnp.transpose(mixed_blocks, (1, 0, 2, 3)).reshape(FRAMES, ROWS, COLS, D)
    lists = jnp.roll(neighbour_list, TILES_WIDE, axis=0).reshape(CLIPS, TILES, SLOTS)
    results = lax.map(clip_pass, (by_clip(spatial_q), by_clip(spatial_k), by_clip(spatial_v), by_clip(residual), lists))
    stacked = jnp.transpose(results, (1, 0, 2, 3, 4)).reshape(FRAMES, CLIPS * ROWS, COLS, D)
    return jnp.roll(stacked, -TILE, axis=1)
```

```python
import math

import jax
import jax.numpy as jnp
from jax import lax
from jax.sharding import PartitionSpec as P

HEADS = 16
TILE = 8
SLOTS = 6
ROWS = 32
BLOCK = 4


EPS = 1e-06


ROW_AXIS = ("x", "zl")
FRAME_AXIS = ("y", "zh", "core")


def padded(block):
    count = lax.axis_size(ROW_AXIS)
    down = [(i, (i + 1) % count) for i in range(count) if (i + 1) % 4 != 3]
    up = [(target, source) for source, target in down]
    low = lax.ppermute(block, ROW_AXIS, down)
    high = lax.ppermute(block, ROW_AXIS, up)
    return jnp.concatenate([low, block, high], axis=2)


def gathered(weight):
    other = lax.ppermute(weight, ("zh", "zl"), [(i, 7 - i) for i in range(8)])
    first = lax.axis_index("zh") == 0
    pair = jnp.stack((jnp.where(first, weight, other), jnp.where(first, other, weight)), 0)
    full = lax.all_gather(pair, ("y", "core"), axis=0, tiled=False)
    rows, cols = weight.shape
    full = full.reshape(4, 2, 2, rows, cols)
    return jnp.transpose(full, (0, 2, 1, 3, 4)).reshape(16 * rows, cols)


def tiles_of(field):
    leading = field.shape[:-3]
    height, breadth, channels = field.shape[-3:]
    tile_grid = field.reshape(leading + (height // TILE, TILE, breadth // TILE, TILE, channels))
    lead_count = len(leading)
    arrangement = tuple(range(lead_count)) + (
        lead_count,
        lead_count + 2,
        lead_count + 1,
        lead_count + 3,
        lead_count + 4,
    )
    tile_grid = jnp.transpose(tile_grid, arrangement)
    return tile_grid.reshape(leading + (height // TILE * (breadth // TILE), TILE * TILE, channels))


def untile(tiles, height, breadth):
    leading = tiles.shape[:-3]
    channels = tiles.shape[-1]
    tile_grid = tiles.reshape(leading + (height // TILE, breadth // TILE, TILE, TILE, channels))
    lead_count = len(leading)
    arrangement = tuple(range(lead_count)) + (
        lead_count,
        lead_count + 2,
        lead_count + 1,
        lead_count + 3,
        lead_count + 4,
    )
    return jnp.transpose(tile_grid, arrangement).reshape(leading + (height, breadth, channels))


def window_attention(queries, keys, values):
    tile_count, token_count, channels = queries.shape
    head_size = channels // HEADS
    shaped_q = queries.reshape(tile_count, token_count, HEADS, head_size)
    shaped_k = keys.reshape(tile_count, -1, HEADS, head_size)
    shaped_v = values.reshape(tile_count, -1, HEADS, head_size)
    scores = jnp.einsum(
        "tqhe,tkhe->thqk", shaped_q, shaped_k, preferred_element_type=jnp.float32
    ) * (1.0 / math.sqrt(head_size))
    peak = jnp.max(scores, axis=-1, keepdims=True)
    powers = jnp.exp(scores - peak)
    weights = (powers / jnp.sum(powers, axis=-1, keepdims=True)).astype(jnp.bfloat16)
    mixed = jnp.einsum("thqk,tkhe->tqhe", weights, shaped_v, preferred_element_type=jnp.float32)
    return mixed.astype(jnp.bfloat16).reshape(tile_count, token_count, channels)


def frame_attention(queries, keys, values, allowed):
    frame_count, spot_count, channels = queries.shape
    head_size = channels // HEADS
    shaped_q = queries.reshape(frame_count, spot_count, HEADS, head_size)
    shaped_k = keys.reshape(frame_count, spot_count, HEADS, head_size)
    shaped_v = values.reshape(frame_count, spot_count, HEADS, head_size)
    scores = jnp.einsum(
        "fphe,gphe->phfg", shaped_q, shaped_k, preferred_element_type=jnp.float32
    ) * (1.0 / math.sqrt(head_size))
    scores = jnp.where(allowed, scores, -jnp.inf)
    peak = jnp.max(scores, axis=-1, keepdims=True)
    powers = jnp.exp(scores - peak)
    weights = (powers / jnp.sum(powers, axis=-1, keepdims=True)).astype(jnp.bfloat16)
    mixed = jnp.einsum("phfg,gphe->fphe", weights, shaped_v, preferred_element_type=jnp.float32)
    return mixed.astype(jnp.bfloat16).reshape(frame_count, spot_count, channels)


def normalize(field, mod_shift, mod_scale):
    average = jnp.mean(field, axis=-1, keepdims=True)
    centred = field - average
    spread = jnp.mean(centred * centred, axis=-1, keepdims=True)
    return centred * lax.rsqrt(spread + EPS) * (1.0 + mod_scale) + mod_shift


def fold_with(left, piece):
    return jnp.dot(left, piece, preferred_element_type=jnp.float32)


def frame_window(items):
    return window_attention(items[0], items[1], items[2])


def local(
    spatial_q,
    spatial_k,
    spatial_v,
    residual,
    neighbour_list,
    block_mask,
    out_weight,
    qkv_weight,
    pos_embed,
    mod_shift,
    mod_scale,
):
    frames_here, height, breadth, channels = spatial_q.shape
    tiles_wide = breadth // TILE
    tokens_here = frames_here * height * breadth
    stacked = jnp.stack((spatial_k, spatial_v), 0)
    rims = padded(stacked)
    key_tiles = tiles_of(rims)
    tile_row_here = (lax.axis_index(ROW_AXIS) + 1) % (ROWS // TILE)
    local_ids = (
        (neighbour_list // tiles_wide - tile_row_here + 1) * tiles_wide
        + neighbour_list % tiles_wide
    ).reshape(-1)
    picked = jnp.take(key_tiles, local_ids, axis=2).reshape(
        2, frames_here, tiles_wide, SLOTS * TILE * TILE, channels
    )
    query_tiles = tiles_of(spatial_q)
    attended = lax.map(frame_window, (query_tiles, picked[0], picked[1]))
    heads = untile(attended, height, breadth).reshape(tokens_here, channels)
    spatial_sum = fold_with(heads, gathered(out_weight))
    mixed = (residual.reshape(tokens_here, channels).astype(jnp.float32) + spatial_sum).astype(
        jnp.bfloat16
    )
    mixed = lax.optimization_barrier(mixed)
    shifted = (
        mixed.astype(jnp.float32).reshape(frames_here, height * breadth, channels)
        + pos_embed[:, None, :]
    )
    normed = normalize(shifted, mod_shift, mod_scale).astype(jnp.bfloat16)
    normed = lax.all_to_all(normed, FRAME_AXIS, split_axis=1, concat_axis=0, tiled=True)
    projected = fold_with(normed.reshape(tokens_here, channels), gathered(qkv_weight)).astype(
        jnp.bfloat16
    )
    projected = projected.reshape(-1, tokens_here // 32, 3 * channels)
    allowed = jnp.repeat(jnp.repeat(block_mask, BLOCK, axis=0), BLOCK, axis=1) == 1
    temporal = frame_attention(
        projected[..., :channels],
        projected[..., channels : 2 * channels],
        projected[..., 2 * channels :],
        allowed,
    )
    returned = lax.all_to_all(temporal, FRAME_AXIS, split_axis=0, concat_axis=1, tiled=True)
    return returned.reshape(frames_here, height, breadth, channels)


def solution(mesh):
    fine = jax.sharding.Mesh(
        mesh.devices.reshape(4, 2, 2, 4, 4), ("y", "zh", "core", "x", "zl")
    )
    tokens = P(FRAME_AXIS, ROW_AXIS, None, None)
    return jax.shard_map(
        local,
        mesh=fine,
        in_specs=(
            tokens,
            tokens,
            tokens,
            tokens,
            P(ROW_AXIS, None),
            P(),
            P(FRAME_AXIS, None),
            P(FRAME_AXIS, None),
            P(FRAME_AXIS, None),
            P(),
            P(),
        ),
        out_specs=tokens,
        check_vma=False,
    )
```

```python
import math

import jax
import jax.numpy as jnp
from jax import lax
from jax.experimental import pallas as pl
from jax.experimental.pallas import tpu as pltpu
from jax.sharding import PartitionSpec as P

HEADS = 16
TILE = 8
SLOTS = 6
BLOCK = 4
TILES_WIDE = 4
D = 1152
HEAD = D // HEADS
EPS = 1e-06
ROW_AXIS = ("x", "zl")
FRAME_AXIS = ("y", "zh", "core")
PAIRS = HEADS // 2
WINDOW = 256
LANES = 128
NT = (((1,), (1,)), ((), ()))
RATE = (1.0 / math.sqrt(HEAD)) * math.log2(math.e)


def pair_masks(pair):
    lane = lax.broadcasted_iota(jnp.int32, (1, WINDOW), 1) + LANES * pair
    first = (lane >= 2 * pair * HEAD) & (lane < (2 * pair + 1) * HEAD)
    second = (lane >= (2 * pair + 1) * HEAD) & (lane < (2 * pair + 2) * HEAD)
    return first, second


def soft(scores):
    peak = jnp.max(scores, axis=-1, keepdims=True)
    powers = jnp.exp2((scores - peak) * RATE)
    total = jnp.sum(powers, axis=-1, keepdims=True)
    return (powers * (1.0 / total)).astype(jnp.bfloat16)


def attend(window_of, bias):
    carried = None
    for pair in range(PAIRS):
        first, second = pair_masks(pair)
        queries, keys, values = window_of(pair)
        rows = queries.shape[0]
        zero = jnp.zeros_like(queries)
        both = jnp.concatenate(
            [jnp.where(first, queries, zero), jnp.where(second, queries, zero)], axis=0
        )
        scores = lax.dot_general(both, keys, NT, preferred_element_type=jnp.float32)
        if bias is not None:
            scores = scores + jnp.concatenate([bias, bias], axis=0)
        weights = soft(scores)
        out = jnp.dot(weights, values, preferred_element_type=jnp.float32)
        out = jnp.where(first, out[:rows], jnp.where(second, out[rows:], 0.0))
        low, high = out[:, :LANES], out[:, LANES:]
        yield pair, low if carried is None else low + carried
        carried = high
    yield PAIRS, carried


def spatial_kernel(
    ids,
    q_ref,
    k_low,
    k_own,
    k_high,
    v_low,
    v_own,
    v_high,
    res_ref,
    w_ref,
    pos_ref,
    shift_ref,
    scale_ref,
    out_ref,
    qt,
    kt,
    vt,
    kw,
    vw,
    heads,
    acc,
):
    size = TILE * TILE

    def tile_up(i, _):
        for dst, base, src in (
            (qt, 0, q_ref),
            (kt, 0, k_low),
            (kt, 4, k_own),
            (kt, 8, k_high),
            (vt, 0, v_low),
            (vt, 4, v_own),
            (vt, 8, v_high),
        ):
            rows = src[pl.ds(2 * i, 2)].astype(jnp.float32)
            for c in range(TILES_WIDE):
                part = rows[:, c * TILE : (c + 1) * TILE, :].reshape(2 * TILE, D)
                dst[base + c, pl.ds(pl.multiple_of(16 * i, 16), 16), :] = part.astype(jnp.bfloat16)
        return 0

    lax.fori_loop(0, TILE // 2, tile_up, 0)

    def column(w, _):
        for slot in range(SLOTS):
            tile = ids[w * SLOTS + slot]
            kw[slot * size : (slot + 1) * size, :] = kt[tile]
            vw[slot * size : (slot + 1) * size, :] = vt[tile]

        def window_of(pair):
            lanes = slice(LANES * pair, LANES * pair + WINDOW)
            return qt[w, :, lanes], kw[:, lanes], vw[:, lanes]

        for block, value in attend(window_of, None):
            heads[pl.ds(pl.multiple_of(w * size, size), size), block * LANES : (block + 1) * LANES] = (
                value.astype(jnp.bfloat16)
            )
        return 0

    lax.fori_loop(0, TILES_WIDE, column, 0)
    acc[...] = jnp.dot(heads[...], w_ref[...], preferred_element_type=jnp.float32)

    def finish(i, _):
        added = jnp.concatenate(
            [
                acc[pl.ds(pl.multiple_of(c * size + 16 * i, 16), 16), :].reshape(2, TILE, D)
                for c in range(TILES_WIDE)
            ],
            axis=1,
        ).reshape(2 * TILES_WIDE * TILE, D)
        left = res_ref[pl.ds(2 * i, 2)].astype(jnp.float32).reshape(2 * TILES_WIDE * TILE, D)
        mixed = (left + added).astype(jnp.bfloat16).astype(jnp.float32)
        shifted = mixed + pos_ref[...]
        average = jnp.mean(shifted, axis=-1, keepdims=True)
        centred = shifted - average
        spread = jnp.mean(centred * centred, axis=-1, keepdims=True)
        normed = centred * lax.rsqrt(spread + EPS) * (1.0 + scale_ref[...]) + shift_ref[...]
        out_ref[pl.ds(2 * i, 2)] = normed.reshape(2, TILES_WIDE * TILE, D).astype(jnp.bfloat16)
        return 0

    lax.fori_loop(0, TILE // 2, finish, 0)


def spatial(frame, ids, q, k_low, k, k_high, v_low, v, v_high, residual, weight, pos, shift, scale):
    height, breadth = q.shape[1:3]
    own = pl.BlockSpec((pl.squeezed, height, breadth, D), lambda g, s: (frame, 0, 0, 0))
    halo = pl.BlockSpec((height, breadth, D), lambda g, s: (0, 0, 0))
    row = pl.BlockSpec((1, D), lambda g, s: (0, 0))
    tokens = height * breadth
    bf16 = jnp.bfloat16
    return pl.pallas_call(
        spatial_kernel,
        out_shape=jax.ShapeDtypeStruct((height, breadth, D), bf16),
        grid_spec=pltpu.PrefetchScalarGridSpec(
            num_scalar_prefetch=1,
            grid=(1,),
            in_specs=[
                own,
                halo,
                own,
                halo,
                halo,
                own,
                halo,
                own,
                pl.BlockSpec((D, D), lambda g, s: (0, 0)),
                row,
                row,
                row,
            ],
            out_specs=halo,
            scratch_shapes=[
                pltpu.VMEM((4, 64, D), bf16),
                pltpu.VMEM((12, 64, D), bf16),
                pltpu.VMEM((12, 64, D), bf16),
                pltpu.VMEM((384, D), bf16),
                pltpu.VMEM((384, D), bf16),
                pltpu.VMEM((tokens, D), bf16),
                pltpu.VMEM((tokens, D), jnp.float32),
            ],
        ),
        compiler_params=pltpu.CompilerParams(vmem_limit_bytes=56 << 20),
        name="spatial",
    )(ids, q, k_low, k, k_high, v_low, v, v_high, residual, weight, pos, shift, scale)


def temporal_kernel(x_ref, w_ref, mask_ref, out_ref, xs, proj, done):
    frames = x_ref.shape[0]
    spots = x_ref.shape[1]
    rows = frames * TILE
    blocks = frames // BLOCK
    r = lax.broadcasted_iota(jnp.int32, (rows, rows), 0)
    c = lax.broadcasted_iota(jnp.int32, (rows, rows), 1)
    near = lax.broadcasted_iota(jnp.int32, (rows, blocks), 0) // (BLOCK * TILE)
    spread = (near == lax.broadcasted_iota(jnp.int32, (rows, blocks), 1)).astype(jnp.bfloat16)
    half = jnp.dot(spread, mask_ref[...], preferred_element_type=jnp.float32).astype(jnp.bfloat16)
    allowed = lax.dot_general(half, spread, NT, preferred_element_type=jnp.float32)
    bias = jnp.where((allowed > 0.5) & (r % TILE == c % TILE), 0.0, -1e30)
    for g in range(spots // TILE):
        part = x_ref[...].astype(jnp.float32)[:, g * TILE : (g + 1) * TILE, :]
        xs[g * rows : (g + 1) * rows, :] = part.reshape(rows, D).astype(jnp.bfloat16)
    proj[...] = jnp.dot(xs[...], w_ref[...], preferred_element_type=jnp.float32).astype(jnp.bfloat16)
    for g in range(spots // TILE):

        def window_of(pair):
            lane = LANES * pair
            here = slice(g * rows, (g + 1) * rows)
            return tuple(proj[here, base + lane : base + lane + WINDOW] for base in (0, D, 2 * D))

        for block, value in attend(window_of, bias):
            done[:, g * TILE : (g + 1) * TILE, block * LANES : (block + 1) * LANES] = value.reshape(
                frames, TILE, LANES
            )
    out_ref[...] = done[...].astype(jnp.bfloat16)


def temporal(x, weight, mask):
    frames, spots, _ = x.shape
    return pl.pallas_call(
        temporal_kernel,
        out_shape=jax.ShapeDtypeStruct(x.shape, jnp.bfloat16),
        scratch_shapes=[
            pltpu.VMEM((frames * spots, D), jnp.bfloat16),
            pltpu.VMEM((frames * spots, 3 * D), jnp.bfloat16),
            pltpu.VMEM((frames, spots, D), jnp.float32),
        ],
        compiler_params=pltpu.CompilerParams(vmem_limit_bytes=56 << 20),
        name="temporal",
    )(x, weight, mask)


def gathered(weight):
    other = lax.ppermute(weight, ("zh", "zl"), [(i, 7 - i) for i in range(8)])
    first = lax.axis_index("zh") == 0
    pair = jnp.stack((jnp.where(first, weight, other), jnp.where(first, other, weight)), 0)
    full = lax.all_gather(pair, ("y", "core"), axis=0, tiled=False)
    rows, cols = weight.shape
    full = full.reshape(4, 2, 2, rows, cols)
    return jnp.transpose(full, (0, 2, 1, 3, 4)).reshape(16 * rows, cols)


def local(
    spatial_q,
    spatial_k,
    spatial_v,
    residual,
    neighbour_list,
    block_mask,
    out_weight,
    qkv_weight,
    pos_embed,
    mod_shift,
    mod_scale,
):
    frames_here, height, breadth, channels = spatial_q.shape
    spots = height * breadth
    count = lax.axis_size(ROW_AXIS)
    down = [(i, (i + 1) % count) for i in range(count) if (i + 1) % 4 != 3]
    up = [(target, source) for source, target in down]
    tile_row_here = (lax.axis_index(ROW_AXIS) + 1) % 4
    ids = (
        (neighbour_list // TILES_WIDE - tile_row_here + 1) * TILES_WIDE
        + neighbour_list % TILES_WIDE
    ).reshape(-1)
    w_out = gathered(out_weight)
    shift = mod_shift.reshape(1, channels)
    scale = mod_scale.reshape(1, channels)
    moved = []
    for f in range(frames_here):
        moved.append(
            [
                lax.ppermute(whole[f], ROW_AXIS, pairs)
                for whole in (spatial_k, spatial_v)
                for pairs in (down, up)
            ]
        )
    w_qkv = gathered(qkv_weight)
    normed = []
    for f in range(frames_here):
        k_low, k_high, v_low, v_high = moved[f]
        normed.append(
            spatial(
                f,
                ids,
                spatial_q,
                k_low,
                spatial_k,
                k_high,
                v_low,
                spatial_v,
                v_high,
                residual,
                w_out,
                pos_embed[f].reshape(1, channels),
                shift,
                scale,
            )
        )
    normed = jnp.stack(normed, 0).reshape(frames_here, spots, channels)
    normed = lax.all_to_all(normed, FRAME_AXIS, split_axis=1, concat_axis=0, tiled=True)
    mixed = temporal(normed, w_qkv, block_mask.astype(jnp.bfloat16))
    returned = lax.all_to_all(mixed, FRAME_AXIS, split_axis=0, concat_axis=1, tiled=True)
    return returned.reshape(frames_here, height, breadth, channels)


def solution(mesh):
    fine = jax.sharding.Mesh(mesh.devices.reshape(4, 2, 2, 4, 4), ("y", "zh", "core", "x", "zl"))
    tokens = P(FRAME_AXIS, ROW_AXIS, None, None)
    return jax.shard_map(
        local,
        mesh=fine,
        in_specs=(
            tokens,
            tokens,
            tokens,
            tokens,
            P(ROW_AXIS, None),
            P(),
            P(FRAME_AXIS, None),
            P(FRAME_AXIS, None),
            P(FRAME_AXIS, None),
            P(),
            P(),
        ),
        out_specs=tokens,
        check_vma=False,
    )
```

```python
import math

import jax
import jax.numpy as jnp
from jax import lax
from jax.experimental import pallas as pl
from jax.experimental.pallas import tpu as pltpu
from jax.sharding import PartitionSpec as P


HEADS = 16
TILE = 8
SLOTS = 6
TILES_WIDE = 4
D = 1152
HEAD = D // HEADS
EPS = 1e-06
ROW_AXIS = ("x", "zl")
FRAME_AXIS = ("y", "zh", "core")
PEERS = 16
PAIRS = HEADS // 2
WINDOW = 256
LANES = 128
NT = (((1,), (1,)), ((), ()))
RATE = (1.0 / math.sqrt(HEAD)) * math.log2(math.e)


def pair_masks(pair):
    lane = lax.broadcasted_iota(jnp.int32, (1, WINDOW), 1) + LANES * pair
    first = (lane >= 2 * pair * HEAD) & (lane < (2 * pair + 1) * HEAD)
    second = (lane >= (2 * pair + 1) * HEAD) & (lane < (2 * pair + 2) * HEAD)
    return first, second


def soft(scores):
    peak = jnp.max(scores, axis=-1, keepdims=True)
    powers = jnp.exp2((scores - peak) * RATE)
    total = jnp.sum(powers, axis=-1, keepdims=True)
    return (powers * (1.0 / total)).astype(jnp.bfloat16)


def attend(window_of, bias):
    carried = None
    for pair in range(PAIRS):
        first, second = pair_masks(pair)
        queries, keys, values = window_of(pair)
        rows = queries.shape[0]
        zero = jnp.zeros_like(queries)
        both = jnp.concatenate(
            [jnp.where(first, queries, zero), jnp.where(second, queries, zero)], axis=0
        )
        scores = lax.dot_general(both, keys, NT, preferred_element_type=jnp.float32)
        if bias is not None:
            scores = scores + jnp.concatenate([bias, bias], axis=0)
        weights = soft(scores)
        out = jnp.dot(weights, values, preferred_element_type=jnp.float32)
        out = jnp.where(first, out[:rows], jnp.where(second, out[rows:], 0.0))
        low, high = out[:, :LANES], out[:, LANES:]
        yield pair, low if carried is None else low + carried
        carried = high
    yield PAIRS, carried


def spatial_kernel(
    ids,
    q_ref,
    k_own,
    v_own,
    low,
    high,
    res_ref,
    w_ref,
    pos_ref,
    shift_ref,
    scale_ref,
    out_ref,
    qt,
    kt,
    vt,
    kw,
    vw,
    heads,
    acc,
):
    size = TILE * TILE

    def tile_up(i, _):
        for dst, base, src in (
            (qt, 0, q_ref),
            (kt, 0, low.at[0]),
            (kt, 4, k_own),
            (kt, 8, high.at[0]),
            (vt, 0, low.at[1]),
            (vt, 4, v_own),
            (vt, 8, high.at[1]),
        ):
            rows = src[pl.ds(2 * i, 2)].astype(jnp.float32)
            for c in range(TILES_WIDE):
                part = rows[:, c * TILE : (c + 1) * TILE, :].reshape(2 * TILE, D)
                dst[base + c, pl.ds(pl.multiple_of(16 * i, 16), 16), :] = part.astype(jnp.bfloat16)
        return 0

    lax.fori_loop(0, TILE // 2, tile_up, 0)

    def column(w, _):
        for slot in range(SLOTS):
            tile = ids[w * SLOTS + slot]
            kw[slot * size : (slot + 1) * size, :] = kt[tile]
            vw[slot * size : (slot + 1) * size, :] = vt[tile]

        def window_of(pair):
            lanes = slice(LANES * pair, LANES * pair + WINDOW)
            return qt[w, :, lanes], kw[:, lanes], vw[:, lanes]

        for block, value in attend(window_of, None):
            heads[pl.ds(pl.multiple_of(w * size, size), size), block * LANES : (block + 1) * LANES] = (
                value.astype(jnp.bfloat16)
            )
        return 0

    lax.fori_loop(0, TILES_WIDE, column, 0)
    acc[...] = jnp.dot(heads[...], w_ref[...], preferred_element_type=jnp.float32)

    def finish(i, _):
        added = jnp.concatenate(
            [
                acc[pl.ds(pl.multiple_of(c * size + 16 * i, 16), 16), :].reshape(2, TILE, D)
                for c in range(TILES_WIDE)
            ],
            axis=1,
        ).reshape(2 * TILES_WIDE * TILE, D)
        left = res_ref[pl.ds(2 * i, 2)].astype(jnp.float32).reshape(2 * TILES_WIDE * TILE, D)
        mixed = (left + added).astype(jnp.bfloat16).astype(jnp.float32)
        shifted = mixed + pos_ref[...]
        average = jnp.mean(shifted, axis=-1, keepdims=True)
        centred = shifted - average
        spread = jnp.mean(centred * centred, axis=-1, keepdims=True)
        normed = centred * lax.rsqrt(spread + EPS) * (1.0 + scale_ref[...]) + shift_ref[...]
        out_ref[pl.ds(2 * i, 2)] = normed.reshape(2, TILES_WIDE * TILE, D).astype(jnp.bfloat16)
        return 0

    lax.fori_loop(0, TILE // 2, finish, 0)


def spatial(frame, ids, q, k, v, low, high, residual, weight, pos, shift, scale):
    height, breadth = q.shape[1:3]
    own = pl.BlockSpec((pl.squeezed, height, breadth, D), lambda g, s: (frame, 0, 0, 0))
    halo = pl.BlockSpec((2, height, breadth, D), lambda g, s: (0, 0, 0, 0))
    row = pl.BlockSpec((1, D), lambda g, s: (0, 0))
    tokens = height * breadth
    bf16 = jnp.bfloat16
    return pl.pallas_call(
        spatial_kernel,
        out_shape=jax.ShapeDtypeStruct((height, breadth, D), bf16),
        grid_spec=pltpu.PrefetchScalarGridSpec(
            num_scalar_prefetch=1,
            grid=(1,),
            in_specs=[
                own,
                own,
                own,
                halo,
                halo,
                own,
                pl.BlockSpec((D, D), lambda g, s: (0, 0)),
                row,
                row,
                row,
            ],
            out_specs=pl.BlockSpec((height, breadth, D), lambda g, s: (0, 0, 0)),
            scratch_shapes=[
                pltpu.VMEM((4, 64, D), bf16),
                pltpu.VMEM((12, 64, D), bf16),
                pltpu.VMEM((12, 64, D), bf16),
                pltpu.VMEM((384, D), bf16),
                pltpu.VMEM((384, D), bf16),
                pltpu.VMEM((tokens, D), bf16),
                pltpu.VMEM((tokens, D), jnp.float32),
            ],
        ),
        compiler_params=pltpu.CompilerParams(vmem_limit_bytes=56 << 20),
        name="spatial",
    )(ids, q, k, v, low, high, residual, weight, pos, shift, scale)


def temporal_kernel(even_ref, odd_ref, w_ref, mask_ref, out_ref, xs, proj, done):
    per_frame = even_ref.shape[0]
    spots = done.shape[1]
    peers = per_frame // spots
    half = peers * TILE
    rows = 2 * half
    blocks = mask_ref.shape[0]
    r = lax.broadcasted_iota(jnp.int32, (rows, rows), 0)
    c = lax.broadcasted_iota(jnp.int32, (rows, rows), 1)
    near = (lax.broadcasted_iota(jnp.int32, (rows, blocks), 0) % half) // (half // blocks)
    spread = (near == lax.broadcasted_iota(jnp.int32, (rows, blocks), 1)).astype(jnp.bfloat16)
    reach = jnp.dot(spread, mask_ref[...], preferred_element_type=jnp.float32).astype(jnp.bfloat16)
    allowed = lax.dot_general(reach, spread, NT, preferred_element_type=jnp.float32)
    bias = jnp.where((allowed > 0.5) & (r % TILE == c % TILE), 0.0, -1e30)
    for f, src in enumerate((even_ref, odd_ref)):
        whole = src[...].astype(jnp.float32).reshape(peers, spots, D)
        for g in range(spots // TILE):
            part = whole[:, g * TILE : (g + 1) * TILE, :].reshape(half, D)
            xs[g * rows + f * half : g * rows + (f + 1) * half, :] = part.astype(jnp.bfloat16)
    proj[...] = jnp.dot(xs[...], w_ref[...], preferred_element_type=jnp.float32).astype(jnp.bfloat16)
    for g in range(spots // TILE):

        def window_of(pair):
            lane = LANES * pair
            here = slice(g * rows, (g + 1) * rows)
            return tuple(proj[here, base + lane : base + lane + WINDOW] for base in (0, D, 2 * D))

        for block, value in attend(window_of, bias):
            done[:, g * TILE : (g + 1) * TILE, block * LANES : (block + 1) * LANES] = value.reshape(
                2 * peers, TILE, LANES
            )
    for f in range(2):
        out_ref[f] = done[f * peers : (f + 1) * peers].reshape(per_frame, D).astype(jnp.bfloat16)


def temporal(even, odd, weight, mask):
    per_frame, _ = even.shape
    peers = PEERS
    spots = per_frame // peers
    return pl.pallas_call(
        temporal_kernel,
        out_shape=jax.ShapeDtypeStruct((2, per_frame, D), jnp.bfloat16),
        scratch_shapes=[
            pltpu.VMEM((2 * per_frame, D), jnp.bfloat16),
            pltpu.VMEM((2 * per_frame, 3 * D), jnp.bfloat16),
            pltpu.VMEM((2 * peers, spots, D), jnp.float32),
        ],
        compiler_params=pltpu.CompilerParams(vmem_limit_bytes=56 << 20),
        name="temporal",
    )(even, odd, weight, mask)


def mirrored(weight):
    return lax.ppermute(weight, ("zh", "zl"), [(i, 7 - i) for i in range(8)])


def gathered(weight, other):
    first = lax.axis_index("zh") == 0
    pair = jnp.stack((jnp.where(first, weight, other), jnp.where(first, other, weight)), 0)
    full = lax.all_gather(pair, ("y", "core"), axis=0, tiled=False)
    rows, cols = weight.shape
    full = full.reshape(4, 2, 2, rows, cols)
    return jnp.transpose(full, (0, 2, 1, 3, 4)).reshape(16 * rows, cols)


def local(
    spatial_q,
    spatial_k,
    spatial_v,
    residual,
    neighbour_list,
    block_mask,
    out_weight,
    qkv_weight,
    pos_embed,
    mod_shift,
    mod_scale,
):
    frames_here, height, breadth, channels = spatial_q.shape
    spots = height * breadth
    count = lax.axis_size(ROW_AXIS)
    down = [(i, (i + 1) % count) for i in range(count) if (i + 1) % 4 != 3]
    up = [(target, source) for source, target in down]
    moved = []
    for f in range(frames_here):
        both = jnp.stack((spatial_k[f], spatial_v[f]), 0)
        low = lax.ppermute(both, ROW_AXIS, down)
        high = lax.ppermute(both, ROW_AXIS, up)
        moved.append((low, high))
    w_out = gathered(out_weight, mirrored(out_weight))
    w_qkv = gathered(qkv_weight, mirrored(qkv_weight))
    tile_row_here = (lax.axis_index(ROW_AXIS) + 1) % 4
    ids = (
        (neighbour_list // TILES_WIDE - tile_row_here + 1) * TILES_WIDE
        + neighbour_list % TILES_WIDE
    ).reshape(-1)
    shift = mod_shift.reshape(1, channels)
    scale = mod_scale.reshape(1, channels)
    arrived = []
    for f in range(frames_here):
        low, high = moved[f]
        if f == frames_here - 1:
            low, w_qkv = lax.optimization_barrier((low, w_qkv))
        normed = spatial(
            f,
            ids,
            spatial_q,
            spatial_k,
            spatial_v,
            low,
            high,
            residual,
            w_out,
            pos_embed[f].reshape(1, channels),
            shift,
            scale,
        ).reshape(spots, channels)
        arrived.append(
            lax.all_to_all(normed, FRAME_AXIS, split_axis=0, concat_axis=0, tiled=True)
        )
    mask = block_mask.astype(jnp.bfloat16)
    done = temporal(arrived[0], arrived[1], w_qkv, mask)
    returned = lax.all_to_all(done, FRAME_AXIS, split_axis=1, concat_axis=1, tiled=True)
    return returned.reshape(frames_here, height, breadth, channels)


def solution(mesh):
    fine = jax.sharding.Mesh(mesh.devices.reshape(4, 2, 2, 4, 4), ("y", "zh", "core", "x", "zl"))
    tokens = P(FRAME_AXIS, ROW_AXIS, None, None)

    return jax.shard_map(
        local,
        mesh=fine,
        in_specs=(
            tokens,
            tokens,
            tokens,
            tokens,
            P(ROW_AXIS, None),
            P(),
            P(FRAME_AXIS, None),
            P(FRAME_AXIS, None),
            P(FRAME_AXIS, None),
            P(),
            P(),
        ),
        out_specs=tokens,
        check_vma=False,
    )
```

```python
import math

import jax
import jax.numpy as jnp
from jax import lax
from jax.experimental import pallas as pl
from jax.experimental.pallas import tpu as pltpu
from jax.sharding import PartitionSpec as P


HEADS = 16
TILE = 8
SLOTS = 6
TILES_WIDE = 4
D = 1152
HEAD = D // HEADS
EPS = 1e-06
ROW_AXIS = ("x", "zl")
FRAME_AXIS = ("y", "zh", "core")
PEERS = 16
PAIRS = HEADS // 2
WINDOW = 256
LANES = 128
CHUNK = 64
NT = (((1,), (1,)), ((), ()))
RATE = (1.0 / math.sqrt(HEAD)) * math.log2(math.e)


def pair_masks(pair):
    lane = lax.broadcasted_iota(jnp.int32, (1, WINDOW), 1) + LANES * pair
    first = (lane >= 2 * pair * HEAD) & (lane < (2 * pair + 1) * HEAD)
    second = (lane >= (2 * pair + 1) * HEAD) & (lane < (2 * pair + 2) * HEAD)
    return first, second


def attend(window_of, bias, scored, weighed):
    rows = scored.shape[1] // 2

    def score(pair):
        first, second = pair_masks(pair)
        queries, keys, _ = window_of(pair)
        zero = jnp.zeros_like(queries)
        for side, mask in enumerate((first, second)):
            scored[pair % 2, side * rows : (side + 1) * rows, :] = lax.dot_general(
                jnp.where(mask, queries, zero), keys, NT, preferred_element_type=jnp.float32
            )

    def soften(pair):
        for at in range(0, 2 * rows, CHUNK):
            scores = scored[pair % 2, at : at + CHUNK, :]
            if bias is not None:
                scores = scores + bias[at % rows : at % rows + CHUNK, :]
            peak = jnp.max(scores, axis=-1, keepdims=True)
            powers = jnp.exp2((scores - peak) * RATE)
            total = jnp.sum(powers, axis=-1, keepdims=True)
            weighed[pair % 2, at : at + CHUNK, :] = (powers * (1.0 / total)).astype(jnp.bfloat16)

    carried = None
    score(0)
    for pair in range(PAIRS + 1):
        if pair + 1 < PAIRS:
            score(pair + 1)
        if pair > 0:
            done = pair - 1
            first, second = pair_masks(done)
            values = window_of(done)[2]
            out = jnp.dot(weighed[done % 2], values, preferred_element_type=jnp.float32)
            out = jnp.where(first, out[:rows], jnp.where(second, out[rows:], 0.0))
            low, high = out[:, :LANES], out[:, LANES:]
            yield done, low if carried is None else low + carried
            carried = high
        if pair < PAIRS:
            soften(pair)
    yield PAIRS, carried


def spatial_kernel(
    ids,
    q_ref,
    k_own,
    v_own,
    low,
    high,
    res_ref,
    w_ref,
    pos_ref,
    shift_ref,
    scale_ref,
    out_ref,
    qt,
    kt,
    vt,
    kw,
    vw,
    heads,
    acc,
    scored,
    weighed,
):
    size = TILE * TILE

    def tile_up(i, _):
        for dst, base, src in (
            (qt, 0, q_ref),
            (kt, 0, low.at[0]),
            (kt, 4, k_own),
            (kt, 8, high.at[0]),
            (vt, 0, low.at[1]),
            (vt, 4, v_own),
            (vt, 8, high.at[1]),
        ):
            rows = src[pl.ds(2 * i, 2)].astype(jnp.float32)
            for c in range(TILES_WIDE):
                part = rows[:, c * TILE : (c + 1) * TILE, :].reshape(2 * TILE, D)
                dst[base + c, pl.ds(pl.multiple_of(16 * i, 16), 16), :] = part.astype(jnp.bfloat16)
        return 0

    lax.fori_loop(0, TILE // 2, tile_up, 0)

    def column(w, _):
        for slot in range(SLOTS):
            tile = ids[w * SLOTS + slot]
            kw[slot * size : (slot + 1) * size, :] = kt[tile]
            vw[slot * size : (slot + 1) * size, :] = vt[tile]

        def window_of(pair):
            lanes = slice(LANES * pair, LANES * pair + WINDOW)
            return qt[w, :, lanes], kw[:, lanes], vw[:, lanes]

        for block, value in attend(window_of, None, scored, weighed):
            heads[pl.ds(pl.multiple_of(w * size, size), size), block * LANES : (block + 1) * LANES] = (
                value.astype(jnp.bfloat16)
            )
        return 0

    lax.fori_loop(0, TILES_WIDE, column, 0)
    acc[...] = jnp.dot(heads[...], w_ref[...], preferred_element_type=jnp.float32)

    def finish(i, _):
        added = jnp.concatenate(
            [
                acc[pl.ds(pl.multiple_of(c * size + 16 * i, 16), 16), :].reshape(2, TILE, D)
                for c in range(TILES_WIDE)
            ],
            axis=1,
        ).reshape(2 * TILES_WIDE * TILE, D)
        left = res_ref[pl.ds(2 * i, 2)].astype(jnp.float32).reshape(2 * TILES_WIDE * TILE, D)
        mixed = (left + added).astype(jnp.bfloat16).astype(jnp.float32)
        shifted = mixed + pos_ref[...]
        average = jnp.mean(shifted, axis=-1, keepdims=True)
        centred = shifted - average
        spread = jnp.mean(centred * centred, axis=-1, keepdims=True)
        normed = centred * lax.rsqrt(spread + EPS) * (1.0 + scale_ref[...]) + shift_ref[...]
        out_ref[pl.ds(2 * i, 2)] = normed.reshape(2, TILES_WIDE * TILE, D).astype(jnp.bfloat16)
        return 0

    lax.fori_loop(0, TILE // 2, finish, 0)


def spatial(frame, ids, q, k, v, low, high, residual, weight, pos, shift, scale):
    height, breadth = q.shape[1:3]
    own = pl.BlockSpec((pl.squeezed, height, breadth, D), lambda g, s: (frame, 0, 0, 0))
    halo = pl.BlockSpec((2, height, breadth, D), lambda g, s: (0, 0, 0, 0))
    row = pl.BlockSpec((1, D), lambda g, s: (0, 0))
    tokens = height * breadth
    bf16 = jnp.bfloat16
    return pl.pallas_call(
        spatial_kernel,
        out_shape=jax.ShapeDtypeStruct((height, breadth, D), bf16),
        grid_spec=pltpu.PrefetchScalarGridSpec(
            num_scalar_prefetch=1,
            grid=(1,),
            in_specs=[
                own,
                own,
                own,
                halo,
                halo,
                own,
                pl.BlockSpec((D, D), lambda g, s: (0, 0)),
                row,
                row,
                row,
            ],
            out_specs=pl.BlockSpec((height, breadth, D), lambda g, s: (0, 0, 0)),
            scratch_shapes=[
                pltpu.VMEM((4, 64, D), bf16),
                pltpu.VMEM((12, 64, D), bf16),
                pltpu.VMEM((12, 64, D), bf16),
                pltpu.VMEM((384, D), bf16),
                pltpu.VMEM((384, D), bf16),
                pltpu.VMEM((tokens, D), bf16),
                pltpu.VMEM((tokens, D), jnp.float32),
                pltpu.VMEM((2, 128, 384), jnp.float32),
                pltpu.VMEM((2, 128, 384), bf16),
            ],
        ),
        compiler_params=pltpu.CompilerParams(vmem_limit_bytes=56 << 20),
        name="spatial",
    )(ids, q, k, v, low, high, residual, weight, pos, shift, scale)


def temporal_kernel(even_ref, odd_ref, w_ref, mask_ref, out_ref, xs, proj, done, bias, scored, weighed):
    per_frame = even_ref.shape[0]
    spots = done.shape[1]
    peers = per_frame // spots
    half = peers * TILE
    rows = 2 * half
    blocks = mask_ref.shape[0]
    r = lax.broadcasted_iota(jnp.int32, (rows, rows), 0)
    c = lax.broadcasted_iota(jnp.int32, (rows, rows), 1)
    near = (lax.broadcasted_iota(jnp.int32, (rows, blocks), 0) % half) // (half // blocks)
    spread = (near == lax.broadcasted_iota(jnp.int32, (rows, blocks), 1)).astype(jnp.bfloat16)
    reach = jnp.dot(spread, mask_ref[...], preferred_element_type=jnp.float32).astype(jnp.bfloat16)
    allowed = lax.dot_general(reach, spread, NT, preferred_element_type=jnp.float32)
    bias[...] = jnp.where((allowed > 0.5) & (r % TILE == c % TILE), 0.0, -1e30)
    for f, src in enumerate((even_ref, odd_ref)):
        whole = src[...].astype(jnp.float32).reshape(peers, spots, D)
        for g in range(spots // TILE):
            part = whole[:, g * TILE : (g + 1) * TILE, :].reshape(half, D)
            xs[g * rows + f * half : g * rows + (f + 1) * half, :] = part.astype(jnp.bfloat16)
    proj[...] = jnp.dot(xs[...], w_ref[...], preferred_element_type=jnp.float32).astype(jnp.bfloat16)
    for g in range(spots // TILE):

        def window_of(pair):
            lane = LANES * pair
            here = slice(g * rows, (g + 1) * rows)
            return tuple(proj[here, base + lane : base + lane + WINDOW] for base in (0, D, 2 * D))

        for block, value in attend(window_of, bias, scored, weighed):
            done[:, g * TILE : (g + 1) * TILE, block * LANES : (block + 1) * LANES] = value.reshape(
                2 * peers, TILE, LANES
            )
    for f in range(2):
        out_ref[:, f] = done[f * peers : (f + 1) * peers].astype(jnp.bfloat16)


def temporal(even, odd, weight, mask):
    per_frame, _ = even.shape
    peers = PEERS
    spots = per_frame // peers
    return pl.pallas_call(
        temporal_kernel,
        out_shape=jax.ShapeDtypeStruct((peers, 2, spots, D), jnp.bfloat16),
        scratch_shapes=[
            pltpu.VMEM((2 * per_frame, D), jnp.bfloat16),
            pltpu.VMEM((2 * per_frame, 3 * D), jnp.bfloat16),
            pltpu.VMEM((2 * peers, spots, D), jnp.float32),
            pltpu.VMEM((256, 256), jnp.float32),
            pltpu.VMEM((2, 512, 256), jnp.float32),
            pltpu.VMEM((2, 512, 256), jnp.bfloat16),
        ],
        compiler_params=pltpu.CompilerParams(vmem_limit_bytes=56 << 20),
        name="temporal",
    )(even, odd, weight, mask)


def mirrored(weight):
    return lax.ppermute(weight, ("zh", "zl"), [(i, 7 - i) for i in range(8)])


def gathered(weight, other):
    first = lax.axis_index("zh") == 0
    pair = jnp.stack((jnp.where(first, weight, other), jnp.where(first, other, weight)), 0)
    full = lax.all_gather(pair, ("y", "core"), axis=0, tiled=False)
    rows, cols = weight.shape
    full = full.reshape(4, 2, 2, rows, cols)
    return jnp.transpose(full, (0, 2, 1, 3, 4)).reshape(16 * rows, cols)


def local(
    spatial_q,
    spatial_k,
    spatial_v,
    residual,
    neighbour_list,
    block_mask,
    out_weight,
    qkv_weight,
    pos_embed,
    mod_shift,
    mod_scale,
):
    frames_here, height, breadth, channels = spatial_q.shape
    spots = height * breadth
    count = lax.axis_size(ROW_AXIS)
    down = [(i, (i + 1) % count) for i in range(count) if (i + 1) % 4 != 3]
    up = [(target, source) for source, target in down]
    moved = []
    for f in range(frames_here):
        both = jnp.stack((spatial_k[f], spatial_v[f]), 0)
        low = lax.ppermute(both, ROW_AXIS, down)
        high = lax.ppermute(both, ROW_AXIS, up)
        moved.append((low, high))
    w_out = gathered(out_weight, mirrored(out_weight))
    w_qkv = gathered(qkv_weight, mirrored(qkv_weight))
    tile_row_here = (lax.axis_index(ROW_AXIS) + 1) % 4
    ids = (
        (neighbour_list // TILES_WIDE - tile_row_here + 1) * TILES_WIDE
        + neighbour_list % TILES_WIDE
    ).reshape(-1)
    shift = mod_shift.reshape(1, channels)
    scale = mod_scale.reshape(1, channels)
    arrived = []
    for f in range(frames_here):
        low, high = moved[f]
        if f == frames_here - 1:
            low, w_qkv = lax.optimization_barrier((low, w_qkv))
        normed = spatial(
            f,
            ids,
            spatial_q,
            spatial_k,
            spatial_v,
            low,
            high,
            residual,
            w_out,
            pos_embed[f].reshape(1, channels),
            shift,
            scale,
        ).reshape(spots, channels)
        arrived.append(
            lax.all_to_all(normed, FRAME_AXIS, split_axis=0, concat_axis=0, tiled=True)
        )
    mask = block_mask.astype(jnp.bfloat16)
    done = temporal(arrived[0], arrived[1], w_qkv, mask)
    returned = lax.all_to_all(done, FRAME_AXIS, split_axis=0, concat_axis=0, tiled=True)
    return jnp.transpose(returned, (1, 0, 2, 3)).reshape(frames_here, height, breadth, channels)


def solution(mesh):
    fine = jax.sharding.Mesh(mesh.devices.reshape(4, 2, 2, 4, 4), ("y", "zh", "core", "x", "zl"))
    tokens = P(FRAME_AXIS, ROW_AXIS, None, None)

    return jax.shard_map(
        local,
        mesh=fine,
        in_specs=(
            tokens,
            tokens,
            tokens,
            tokens,
            P(ROW_AXIS, None),
            P(),
            P(FRAME_AXIS, None),
            P(FRAME_AXIS, None),
            P(FRAME_AXIS, None),
            P(),
            P(),
        ),
        out_specs=tokens,
        check_vma=False,
    )
```

```python
import math

import jax
import jax.numpy as jnp
from jax import lax
from jax.experimental import pallas as pl
from jax.experimental.pallas import tpu as pltpu
from jax.sharding import PartitionSpec as P


HEADS = 16
TILE = 8
SLOTS = 6
TILES_WIDE = 4
D = 1152
HEAD = D // HEADS
EPS = 1e-06
ROW_AXIS = ("x", "zl")
FRAME_AXIS = ("y", "zh", "core")
PEERS = 16
PAIRS = HEADS // 2
WINDOW = 256
LANES = 128
CHUNK = 64
NT = (((1,), (1,)), ((), ()))
RATE = (1.0 / math.sqrt(HEAD)) * math.log2(math.e)


def pair_masks(pair):
    lane = lax.broadcasted_iota(jnp.int32, (1, WINDOW), 1) + LANES * pair
    first = (lane >= 2 * pair * HEAD) & (lane < (2 * pair + 1) * HEAD)
    second = (lane >= (2 * pair + 1) * HEAD) & (lane < (2 * pair + 2) * HEAD)
    return first, second


def attend(window_of, bias, scored, weighed):
    rows = scored.shape[1] // 2

    def score(pair):
        first, second = pair_masks(pair)
        queries, keys, _ = window_of(pair)
        zero = jnp.zeros_like(queries)
        for side, mask in enumerate((first, second)):
            scored[pair % 2, side * rows : (side + 1) * rows, :] = lax.dot_general(
                jnp.where(mask, queries, zero), keys, NT, preferred_element_type=jnp.float32
            )

    def soften(pair):
        for at in range(0, 2 * rows, CHUNK):
            scores = scored[pair % 2, at : at + CHUNK, :]
            if bias is not None:
                scores = scores + bias[at % rows : at % rows + CHUNK, :]
            peak = jnp.max(scores, axis=-1, keepdims=True)
            powers = jnp.exp2((scores - peak) * RATE)
            total = jnp.sum(powers, axis=-1, keepdims=True)
            weighed[pair % 2, at : at + CHUNK, :] = (powers * (1.0 / total)).astype(jnp.bfloat16)

    carried = None
    score(0)
    for pair in range(PAIRS + 1):
        if pair + 1 < PAIRS:
            score(pair + 1)
        if pair > 0:
            done = pair - 1
            first, second = pair_masks(done)
            values = window_of(done)[2]
            out = jnp.dot(weighed[done % 2], values, preferred_element_type=jnp.float32)
            out = jnp.where(first, out[:rows], jnp.where(second, out[rows:], 0.0))
            low, high = out[:, :LANES], out[:, LANES:]
            yield done, low if carried is None else low + carried
            carried = high
        if pair < PAIRS:
            soften(pair)
    yield PAIRS, carried


def spatial_kernel(
    ids,
    q_ref,
    k_own,
    v_own,
    low,
    high,
    res_ref,
    w_ref,
    pos_ref,
    shift_ref,
    scale_ref,
    out_ref,
    qt,
    kt,
    vt,
    kw,
    vw,
    heads,
    acc,
    scored,
    weighed,
    w_buf,
    sem,
):
    size = TILE * TILE
    fetch = pltpu.make_async_copy(w_ref, w_buf, sem)
    fetch.start()

    def tile_up(i, _):
        for dst, base, src in (
            (qt, 0, q_ref),
            (kt, 0, low.at[0]),
            (kt, 4, k_own),
            (kt, 8, high.at[0]),
            (vt, 0, low.at[1]),
            (vt, 4, v_own),
            (vt, 8, high.at[1]),
        ):
            rows = src[pl.ds(2 * i, 2)].astype(jnp.float32)
            for c in range(TILES_WIDE):
                part = rows[:, c * TILE : (c + 1) * TILE, :].reshape(2 * TILE, D)
                dst[base + c, pl.ds(pl.multiple_of(16 * i, 16), 16), :] = part.astype(jnp.bfloat16)
        return 0

    lax.fori_loop(0, TILE // 2, tile_up, 0)

    def column(w, _):
        for slot in range(SLOTS):
            tile = ids[w * SLOTS + slot]
            kw[slot * size : (slot + 1) * size, :] = kt[tile]
            vw[slot * size : (slot + 1) * size, :] = vt[tile]

        def window_of(pair):
            lanes = slice(LANES * pair, LANES * pair + WINDOW)
            return qt[w, :, lanes], kw[:, lanes], vw[:, lanes]

        for block, value in attend(window_of, None, scored, weighed):
            heads[pl.ds(pl.multiple_of(w * size, size), size), block * LANES : (block + 1) * LANES] = (
                value.astype(jnp.bfloat16)
            )
        return 0

    lax.fori_loop(0, TILES_WIDE, column, 0)
    fetch.wait()
    acc[...] = jnp.dot(heads[...], w_buf[...], preferred_element_type=jnp.float32)

    def finish(i, _):
        added = jnp.concatenate(
            [
                acc[pl.ds(pl.multiple_of(c * size + 16 * i, 16), 16), :].reshape(2, TILE, D)
                for c in range(TILES_WIDE)
            ],
            axis=1,
        ).reshape(2 * TILES_WIDE * TILE, D)
        left = res_ref[pl.ds(2 * i, 2)].astype(jnp.float32).reshape(2 * TILES_WIDE * TILE, D)
        mixed = (left + added).astype(jnp.bfloat16).astype(jnp.float32)
        shifted = mixed + pos_ref[...]
        average = jnp.mean(shifted, axis=-1, keepdims=True)
        centred = shifted - average
        spread = jnp.mean(centred * centred, axis=-1, keepdims=True)
        normed = centred * lax.rsqrt(spread + EPS) * (1.0 + scale_ref[...]) + shift_ref[...]
        out_ref[pl.ds(2 * i, 2)] = normed.reshape(2, TILES_WIDE * TILE, D).astype(jnp.bfloat16)
        return 0

    lax.fori_loop(0, TILE // 2, finish, 0)


def spatial(frame, ids, q, k, v, low, high, residual, weight, pos, shift, scale):
    height, breadth = q.shape[1:3]
    own = pl.BlockSpec((pl.squeezed, height, breadth, D), lambda g, s: (frame, 0, 0, 0))
    halo = pl.BlockSpec((2, height, breadth, D), lambda g, s: (0, 0, 0, 0))
    row = pl.BlockSpec((1, D), lambda g, s: (0, 0))
    tokens = height * breadth
    bf16 = jnp.bfloat16
    return pl.pallas_call(
        spatial_kernel,
        out_shape=jax.ShapeDtypeStruct((height, breadth, D), bf16),
        grid_spec=pltpu.PrefetchScalarGridSpec(
            num_scalar_prefetch=1,
            grid=(1,),
            in_specs=[
                own,
                own,
                own,
                halo,
                halo,
                own,
                pl.BlockSpec(memory_space=pl.ANY),
                row,
                row,
                row,
            ],
            out_specs=pl.BlockSpec((height, breadth, D), lambda g, s: (0, 0, 0)),
            scratch_shapes=[
                pltpu.VMEM((4, 64, D), bf16),
                pltpu.VMEM((12, 64, D), bf16),
                pltpu.VMEM((12, 64, D), bf16),
                pltpu.VMEM((384, D), bf16),
                pltpu.VMEM((384, D), bf16),
                pltpu.VMEM((tokens, D), bf16),
                pltpu.VMEM((tokens, D), jnp.float32),
                pltpu.VMEM((2, 128, 384), jnp.float32),
                pltpu.VMEM((2, 128, 384), bf16),
                pltpu.VMEM((D, D), bf16),
                pltpu.SemaphoreType.DMA(()),
            ],
        ),
        compiler_params=pltpu.CompilerParams(vmem_limit_bytes=56 << 20),
        name="spatial",
    )(ids, q, k, v, low, high, residual, weight, pos, shift, scale)


def temporal_kernel(even_ref, odd_ref, w_ref, mask_ref, out_ref, xs, proj, done, bias, scored, weighed, w_buf, sems):
    fetches = [pltpu.make_async_copy(w_ref.at[i], w_buf.at[i], sems.at[i]) for i in range(3)]
    for fetch in fetches:
        fetch.start()
    per_frame = even_ref.shape[0]
    spots = done.shape[1]
    peers = per_frame // spots
    half = peers * TILE
    rows = 2 * half
    blocks = mask_ref.shape[0]
    r = lax.broadcasted_iota(jnp.int32, (rows, rows), 0)
    c = lax.broadcasted_iota(jnp.int32, (rows, rows), 1)
    near = (lax.broadcasted_iota(jnp.int32, (rows, blocks), 0) % half) // (half // blocks)
    spread = (near == lax.broadcasted_iota(jnp.int32, (rows, blocks), 1)).astype(jnp.bfloat16)
    reach = jnp.dot(spread, mask_ref[...], preferred_element_type=jnp.float32).astype(jnp.bfloat16)
    allowed = lax.dot_general(reach, spread, NT, preferred_element_type=jnp.float32)
    bias[...] = jnp.where((allowed > 0.5) & (r % TILE == c % TILE), 0.0, -1e30)
    for f, src in enumerate((even_ref, odd_ref)):
        whole = src[...].astype(jnp.float32).reshape(peers, spots, D)
        for g in range(spots // TILE):
            part = whole[:, g * TILE : (g + 1) * TILE, :].reshape(half, D)
            xs[g * rows + f * half : g * rows + (f + 1) * half, :] = part.astype(jnp.bfloat16)
    for i, fetch in enumerate(fetches):
        fetch.wait()
        proj[:, i * D : (i + 1) * D] = jnp.dot(
            xs[...], w_buf[i], preferred_element_type=jnp.float32
        ).astype(jnp.bfloat16)
    for g in range(spots // TILE):

        def window_of(pair):
            lane = LANES * pair
            here = slice(g * rows, (g + 1) * rows)
            return tuple(proj[here, base + lane : base + lane + WINDOW] for base in (0, D, 2 * D))

        for block, value in attend(window_of, bias, scored, weighed):
            done[:, g * TILE : (g + 1) * TILE, block * LANES : (block + 1) * LANES] = value.reshape(
                2 * peers, TILE, LANES
            )
    for f in range(2):
        out_ref[:, f] = done[f * peers : (f + 1) * peers].astype(jnp.bfloat16)


def temporal(even, odd, weight, mask):
    per_frame, _ = even.shape
    peers = PEERS
    spots = per_frame // peers
    return pl.pallas_call(
        temporal_kernel,
        out_shape=jax.ShapeDtypeStruct((peers, 2, spots, D), jnp.bfloat16),
        scratch_shapes=[
            pltpu.VMEM((2 * per_frame, D), jnp.bfloat16),
            pltpu.VMEM((2 * per_frame, 3 * D), jnp.bfloat16),
            pltpu.VMEM((2 * peers, spots, D), jnp.float32),
            pltpu.VMEM((256, 256), jnp.float32),
            pltpu.VMEM((2, 512, 256), jnp.float32),
            pltpu.VMEM((2, 512, 256), jnp.bfloat16),
            pltpu.VMEM((3, D, D), jnp.bfloat16),
            pltpu.SemaphoreType.DMA((3,)),
        ],
        in_specs=[
            pl.BlockSpec(memory_space=pltpu.VMEM),
            pl.BlockSpec(memory_space=pltpu.VMEM),
            pl.BlockSpec(memory_space=pl.ANY),
            pl.BlockSpec(memory_space=pltpu.VMEM),
        ],
        compiler_params=pltpu.CompilerParams(vmem_limit_bytes=56 << 20),
        name="temporal",
    )(even, odd, weight, mask)


def gathered(out_weight, qkv_weight):
    rows, channels = out_weight.shape
    at = lax.axis_index("x") * channels
    every = jnp.concatenate((out_weight, qkv_weight), axis=1)
    mine = lax.dynamic_slice_in_dim(every, at, channels, axis=1)
    other = lax.ppermute(mine, ("zh", "zl"), [(i, 7 - i) for i in range(8)])
    first = lax.axis_index("zh") == 0
    pair = jnp.stack((jnp.where(first, mine, other), jnp.where(first, other, mine)), 0)
    full = lax.all_gather(pair, ("x", "y", "core"), axis=0, tiled=False)
    full = full.reshape(4, 4, 2, 2, rows, channels)
    grouped = [jnp.transpose(part, (0, 1, 3, 2, 4, 5)) for part in (full[:1], full[1:])]
    return grouped[0].reshape(channels, channels), grouped[1].reshape(3, channels, channels)


def local(
    spatial_q,
    spatial_k,
    spatial_v,
    residual,
    neighbour_list,
    block_mask,
    out_weight,
    qkv_weight,
    pos_embed,
    mod_shift,
    mod_scale,
):
    frames_here, height, breadth, channels = spatial_q.shape
    spots = height * breadth
    count = lax.axis_size(ROW_AXIS)
    down = [(i, (i + 1) % count) for i in range(count) if (i + 1) % 4 != 3]
    up = [(target, source) for source, target in down]
    moved = []
    for f in range(frames_here):
        both = jnp.stack((spatial_k[f], spatial_v[f]), 0)
        low = lax.ppermute(both, ROW_AXIS, down)
        high = lax.ppermute(both, ROW_AXIS, up)
        moved.append((low, high))
    w_out, w_qkv = gathered(out_weight, qkv_weight)
    tile_row_here = (lax.axis_index(ROW_AXIS) + 1) % 4
    ids = (
        (neighbour_list // TILES_WIDE - tile_row_here + 1) * TILES_WIDE
        + neighbour_list % TILES_WIDE
    ).reshape(-1)
    shift = mod_shift.reshape(1, channels)
    scale = mod_scale.reshape(1, channels)
    arrived = []
    for f in range(frames_here):
        low, high = moved[f]
        if f == frames_here - 1:
            low, w_qkv = lax.optimization_barrier((low, w_qkv))
        normed = spatial(
            f,
            ids,
            spatial_q,
            spatial_k,
            spatial_v,
            low,
            high,
            residual,
            w_out,
            pos_embed[f].reshape(1, channels),
            shift,
            scale,
        ).reshape(spots, channels)
        arrived.append(
            lax.all_to_all(normed, FRAME_AXIS, split_axis=0, concat_axis=0, tiled=True)
        )
    mask = block_mask.astype(jnp.bfloat16)
    done = temporal(arrived[0], arrived[1], w_qkv, mask)
    returned = lax.all_to_all(done, FRAME_AXIS, split_axis=0, concat_axis=0, tiled=True)
    return jnp.transpose(returned, (1, 0, 2, 3)).reshape(frames_here, height, breadth, channels)


def solution(mesh):
    fine = jax.sharding.Mesh(mesh.devices.reshape(4, 2, 2, 4, 4), ("y", "zh", "core", "x", "zl"))
    tokens = P(FRAME_AXIS, ROW_AXIS, None, None)

    return jax.shard_map(
        local,
        mesh=fine,
        in_specs=(
            tokens,
            tokens,
            tokens,
            tokens,
            P(ROW_AXIS, None),
            P(),
            P(FRAME_AXIS, None),
            P(FRAME_AXIS, None),
            P(FRAME_AXIS, None),
            P(),
            P(),
        ),
        out_specs=tokens,
        check_vma=False,
    )
```
